32 devices in a mesh: section: 2 (over core), ctx: 4 (over y, x), tp: 4 (over z).
Axes of the slice: x: 2, y: 2, z: 4, core: 2. Of those that a mesh axis runs over, the one named last changes fastest.
Arguments:
- inputs: bfloat16 [4, 1024, 2048], P(None, ('ctx', 'tp')), may hold values from -6 to 6
- segments: int32 [4, 1024], replicated, may hold values from 0 to 3, never falling along the last dimension, each value on 1 to 512 neighbouring positions
- cotangent: bfloat16 [4, 1024, 2048], P(None, ('ctx', 'tp')), may hold values from -6 to 6
- ln_gain: bfloat16 [2, 2048], P('section'), may hold values from 0.5 to 1.5
- ln_bias: bfloat16 [2, 2048], P('section'), may hold values from -3 to 3
- qkv_weight: bfloat16 [2, 3, 2048, 2048], P('section', None, None, 'tp'), may hold values from -1 to 1, as said below
- qkv_bias: bfloat16 [2, 3, 2048], P('section', None, 'tp'), may hold values from -3 to 3
- dense_weight: bfloat16 [2, 2048, 2048], P('section', 'tp'), may hold values from -0.75 to 0.75
- fc1_weight: bfloat16 [2, 2048, 8192], P('section', None, 'tp'), may hold values from -0.125 to 0.125
- fc1_bias: bfloat16 [2, 8192], P('section', 'tp'), may hold values from -3 to 3
- fc2_weight: bfloat16 [2, 8192, 2048], P('section', 'tp'), may hold values from -0.0625 to 0.0625
- out_bias: bfloat16 [2, 2048], P('section'), may hold values from -3 to 3
Outputs:
- layer_outputs: bfloat16 [2, 4, 1024, 2048], P('section', None, ('ctx', 'tp'))
- input_grads: bfloat16 [2, 4, 1024, 2048], P('section', None, ('ctx', 'tp'))
- ln_gain_grad: float32 [2, 2048], P('section')
- ln_bias_grad: float32 [2, 2048], P('section')
- qkv_weight_grad: float32 [2, 3, 2048, 2048], P('section', None, None, 'tp')
- qkv_bias_grad: float32 [2, 3, 2048], P('section', None, 'tp')
- dense_weight_grad: float32 [2, 2048, 2048], P('section', 'tp')
- fc1_weight_grad: float32 [2, 2048, 8192], P('section', None, 'tp')
- fc1_bias_grad: float32 [2, 8192], P('section', 'tp')
- fc2_weight_grad: float32 [2, 8192, 2048], P('section', 'tp')
- out_bias_grad: float32 [2, 2048], P('section')
The draws below stay inside these ranges and needn't reach their ends.
Inputs may be any that keep to these rules, and one draw needn't show every extreme that they name: `segments`: within a sequence the ids never fall; each of the 4 documents has 1 to 512 tokens, one exactly 512. `qkv_weight`: entries of order 2048^(-1/2).
All inputs are finite; a program needn't handle non-finite values.
Results may differ from the reference program's by a relative error of at most 0.02.
Values may be sent and summed in bfloat16 or wider, within the bound.
No kernel may reach another device: no remote copies, remote signals or barrier semaphores. Data moves between devices by JAX's collectives and lax.ppermute only.
A program may use at most 640 MiB of HBM per device.

```python
import math
import jax
import jax.numpy as jnp
import numpy as np
from jax import lax

D = 2048
HEADS = 32
HEAD = 64
ROT = 32
FF = 8192
MB = 4
DOCS = 4
LAYERS = 2
SEQ_LEN = 1024


def draw_qkv_weight(key, part):
    normal_part = jax.random.truncated_normal(jax.random.fold_in(key, 11), -5.0, 5.0, (LAYERS, 3, D, D), jnp.float32) * D ** (-0.5)
    return normal_part.astype(jnp.bfloat16)


def shard_levels(rng, dims, pieces, low, largest):
    level = 1.0
    for dim, parts in pieces:
        heights = jax.random.uniform(jax.random.fold_in(jax.random.fold_in(rng, 6), dim), (parts,), jnp.float32, low / len(pieces), largest / len(pieces))
        level = level * jnp.repeat(jnp.exp(heights), dims[dim] // parts).reshape((-1,) + (1,) * (len(dims) - 1 - dim))
    return level


def profile(amount, total, bound, lean):
    weights = [(1 << 20) // math.isqrt(grade ** lean) + 1 for grade in range(2, amount + 1)]
    rest, given = total - bound - (amount - 1), [1] * (amount - 1)
    while rest > 0:
        movable = [i for i in range(amount - 1) if given[i] < bound]
        mass, remaining = sum([weights[i] for i in movable]), rest
        for i in movable:
            extra = min(bound - given[i], max(1, remaining * weights[i] // mass), rest)
            given[i] = given[i] + extra
            rest = rest - extra
    return np.array([bound] + given)


def ragged(own_key, amount, total, bound, skew):
    if amount == 2:
        one = jax.random.randint(own_key, (), max(1, total - bound), min(bound, total - 1) + 1)
        return jnp.stack([one, total - one])
    tallies = jnp.asarray(profile(amount, total, bound, skew), jnp.int32)
    pairs = (amount - 1) // 2
    giver, receiver = tallies[1:1 + 2 * pairs:2], tallies[2:2 + 2 * pairs:2]
    slack = jnp.minimum(giver - 1, bound - receiver)
    shifted = jax.random.randint(jax.random.fold_in(own_key, 1), (pairs,), 0, 1 << 20) % (slack + 1)
    tallies = tallies.at[1:1 + 2 * pairs:2].set(giver - shifted).at[2:2 + 2 * pairs:2].set(receiver + shifted)
    return tallies[jax.random.permutation(jax.random.fold_in(own_key, 2), amount)]


def gaussian(key, shape, width, reach, pieces=(), kind=jnp.bfloat16):
    result = width * jax.random.normal(key, shape, jnp.float32)
    if pieces:
        result = result * shard_levels(key, shape, pieces, -0.22, 0.18)
    return jnp.clip(result, -reach, reach).astype(kind)


def setup_inputs(seed: int = 0) -> dict:
    key_list = jax.random.split(jax.random.key(seed), 13)
    inputs = gaussian(key_list[0], (MB, SEQ_LEN, D), 1.0, 6.0, ((1, 16),))
    segments = jax.vmap(lambda own: jnp.searchsorted(jnp.cumsum(ragged(own, DOCS, SEQ_LEN, SEQ_LEN // 2, 0)), jnp.arange(SEQ_LEN), side="right"))(jax.random.split(key_list[1], MB)).reshape((MB, SEQ_LEN)).astype(jnp.int32)
    cotangent = gaussian(key_list[2], (MB, SEQ_LEN, D), 1.0, 6.0, ((1, 16),))
    ln_gain = jnp.clip(1.0 + 0.1 * jax.random.normal(key_list[3], (LAYERS, D), jnp.float32), 0.5, 1.5).astype(jnp.bfloat16)
    ln_bias = gaussian(key_list[4], (LAYERS, D), 0.5, 3.0, ((0, 2),))
    qkv_weight = draw_qkv_weight(jax.random.fold_in(key_list[12], 71), 0)
    qkv_bias = gaussian(key_list[6], (LAYERS, 3, D), 0.5, 3.0, ((0, 2), (2, 4)))
    dense_weight = gaussian(key_list[7], (LAYERS, D, D), (D // 32) ** -0.5, 0.75, ((0, 2), (1, 4)))
    fc1_weight = gaussian(key_list[8], (LAYERS, D, FF), D ** -0.5, 0.125, ((0, 2), (2, 4)))
    fc1_bias = gaussian(key_list[9], (LAYERS, FF), 0.5, 3.0, ((0, 2), (1, 4)))
    fc2_weight = gaussian(key_list[10], (LAYERS, FF, D), FF ** -0.5, 0.0625, ((0, 2), (1, 4)))
    out_bias = gaussian(key_list[11], (LAYERS, D), 0.5, 3.0, ((0, 2),))
    return dict(inputs=inputs, segments=segments, cotangent=cotangent, ln_gain=ln_gain, ln_bias=ln_bias, qkv_weight=qkv_weight, qkv_bias=qkv_bias, dense_weight=dense_weight, fc1_weight=fc1_weight, fc1_bias=fc1_bias, fc2_weight=fc2_weight, out_bias=out_bias)


EPSILON = 1e-05
NEGATIVE = -1e+30
HIGHEST = lax.Precision.HIGHEST

@jax.custom_vjp
def low(v):
    return lax.optimization_barrier(v.astype(jnp.bfloat16)).astype(jnp.float32)

@jax.custom_vjp
def low_back(v):
    return v

def low_keep(v):
    return (low(v), None)

def low_pass(kept, grad):
    return (grad,)

def back_keep(v):
    return (v, None)

def back_low(kept, grad):
    return (low(grad),)
low.defvjp(low_keep, low_pass)
low_back.defvjp(back_keep, back_low)

def rope_tables(positions, rot_dims):
    half_dims = rot_dims // 2
    frequency = 10000.0 ** (-(2.0 * jnp.arange(half_dims, dtype=jnp.float32)) / rot_dims)
    angles = positions.astype(jnp.float32)[:, None] * frequency[None, :]
    return (jnp.cos(angles)[:, None, :], jnp.sin(angles)[:, None, :])

def rotate(values_in, cosine, sine, rot_dims):
    half_dims = rot_dims // 2
    lower_half = values_in[..., :half_dims]
    upper_half = values_in[..., half_dims:rot_dims]
    return jnp.concatenate([lower_half * cosine - upper_half * sine, upper_half * cosine + lower_half * sine, values_in[..., rot_dims:]], axis=-1)

def attend(queries, keys_in, values_in, documents):
    length = queries.shape[0]
    block_rows = min(512, length)
    blocks = length // block_rows
    key_pos = jnp.arange(length, dtype=jnp.int32)

    def query_block(block_data):
        block_queries, first_row = block_data
        row_pos = first_row + jnp.arange(block_rows, dtype=jnp.int32)
        row_docs = lax.dynamic_slice_in_dim(documents, first_row, block_rows)
        allowed = (key_pos[None, :] <= row_pos[:, None]) & (documents[None, :] == row_docs[:, None])
        scores = jnp.einsum('qhd,khd->hqk', block_queries, keys_in, precision=HIGHEST) * HEAD ** (-0.5)
        scores = jnp.where(allowed[None], low_back(scores), NEGATIVE)
        row_top = lax.optimization_barrier(jnp.max(scores, axis=2, keepdims=True))
        exponent = jnp.exp(scores - row_top)
        probs = low(exponent / lax.optimization_barrier(jnp.sum(exponent, axis=2, keepdims=True)))
        return jnp.einsum('hqk,khd->qhd', probs, values_in, precision=HIGHEST)
    starts = jnp.arange(blocks, dtype=jnp.int32) * block_rows
    results = lax.map(jax.checkpoint(query_block), (queries.reshape(blocks, block_rows, HEADS, HEAD), starts))
    return results.reshape(length, HEADS * HEAD)

def block_forward(x, layer_index, weights, documents):
    gain, shift, w_qkv, b_qkv, w_dense, w_first, b_first, w_second, b_out = weights
    centered = x - lax.optimization_barrier(jnp.mean(x, axis=1, keepdims=True))
    inv_std = lax.rsqrt(lax.optimization_barrier(jnp.mean(centered * centered, axis=1, keepdims=True)) + EPSILON)
    normed = low(centered * inv_std * gain[layer_index] + shift[layer_index])

    def project(matrix, bias):
        return jnp.dot(normed, matrix, precision=HIGHEST) + bias
    length = x.shape[0]
    query_pre = low_back(project(w_qkv[layer_index, 0], b_qkv[layer_index, 0]))
    key_pre = low_back(project(w_qkv[layer_index, 1], b_qkv[layer_index, 1]))
    value_pre = low_back(project(w_qkv[layer_index, 2], b_qkv[layer_index, 2]))
    up_pre = low_back(project(w_first[layer_index], b_first[layer_index]))
    cosine, sine = rope_tables(jnp.arange(length, dtype=jnp.int32), ROT)
    queries = low(rotate(query_pre.reshape(length, HEADS, HEAD), cosine, sine, ROT))
    keys_r = low(rotate(key_pre.reshape(length, HEADS, HEAD), cosine, sine, ROT))
    values_r = low(value_pre.reshape(length, HEADS, HEAD))
    attended = low_back(low(attend(queries, keys_r, values_r, documents)))
    gelu_out = low(jax.nn.gelu(up_pre, approximate=True))
    branch = low_back(jnp.dot(attended, w_dense[layer_index], precision=HIGHEST) + jnp.dot(gelu_out, w_second[layer_index], precision=HIGHEST))
    return x + branch + b_out[layer_index]

def reference(inputs, segments, cotangent, ln_gain, ln_bias, qkv_weight, qkv_bias, dense_weight, fc1_weight, fc1_bias, fc2_weight, out_bias):
    params = tuple((array.astype(jnp.float32) for array in (ln_gain, ln_bias, qkv_weight, qkv_bias, dense_weight, fc1_weight, fc1_bias, fc2_weight, out_bias)))
    layers = ln_gain.shape[0]
    length = inputs.shape[1]

    def network(x, weights, probes, documents):
        results = []
        current = x
        for layer_index in range(layers):
            current = block_forward(current, layer_index, weights, documents)
            results.append(current)
            if layer_index + 1 < layers:
                current = low_back(low(current) + probes[layer_index])
        return tuple(results)

    def per_batch(totals, batch_data):
        x_in, documents, cot_in = batch_data
        probes = jnp.zeros((layers - 1, length, D), jnp.float32)
        results, pullback = jax.vjp(lambda a, b, c: network(a, b, c, documents), x_in.astype(jnp.float32), params, probes)
        cotangents = tuple((jnp.zeros_like(item) for item in results[:-1])) + (cot_in.astype(jnp.float32),)
        grad_x, grad_params, grad_probes = pullback(cotangents)
        totals = jax.tree.map(jnp.add, totals, grad_params)
        return (totals, (jnp.stack(results), jnp.concatenate([grad_x[None], grad_probes], axis=0)))
    zero_grads = jax.tree.map(jnp.zeros_like, params)
    totals, (results, gradients) = lax.scan(per_batch, zero_grads, (inputs, segments, cotangent))
    layer_outputs = jnp.swapaxes(results, 0, 1).astype(jnp.bfloat16)
    input_grads = jnp.swapaxes(gradients, 0, 1).astype(jnp.bfloat16)
    return (layer_outputs, input_grads, totals[0], totals[1], totals[2], totals[3], totals[4], totals[5], totals[6], totals[7], totals[8])
```

```python
import functools

import jax
import jax.numpy as jnp
from jax import lax
from jax.experimental import pallas as pl
from jax.experimental.pallas import tpu as pltpu
from jax.sharding import PartitionSpec as P

HEAD = 64
ROT = 32
PAIR = 2 * HEAD

EPSILON = 1e-05
NEGATIVE = -1e30
GELU_ROOT = 0.7978845608028654
GELU_CUBE = 0.044715

BF = jnp.bfloat16
F32 = jnp.float32
NT = (((1,), (1,)), ((), ()))
TN = (((0,), (0,)), ((), ()))
VMEM_LIMIT = 60 * 1024 * 1024


def sds(shape, dtype):
    return jax.ShapeDtypeStruct(shape, dtype)


def nbytes(*arrays):
    return sum(a.size * a.dtype.itemsize for a in arrays)


def call(kernel, grid, scalars, ins, in_specs, outs, out_specs, flops, name, scratch=(), moved=None):
    return pl.pallas_call(
        kernel,
        grid_spec=pltpu.PrefetchScalarGridSpec(
            num_scalar_prefetch=len(scalars),
            grid=grid,
            in_specs=in_specs,
            out_specs=out_specs,
            scratch_shapes=scratch,
        ),
        out_shape=outs,
        name=name,
        cost_estimate=pl.CostEstimate(
            flops=int(flops),
            bytes_accessed=int(moved if moved is not None else nbytes(*ins) + nbytes(*jax.tree.leaves(outs))),
            transcendentals=0,
        ),
        compiler_params=pltpu.CompilerParams(vmem_limit_bytes=VMEM_LIMIT),
    )(*scalars, *ins)


def dot(a, b, dims=(((1,), (0,)), ((), ()))):
    return lax.dot_general(a, b, dims, preferred_element_type=F32)


def whole(shape):
    return pl.BlockSpec(shape, lambda *_: (0,) * len(shape))


def picked(shape, which, index):
    def index_map(*args):
        ids, sel = args[:-1], args[-1]
        return tuple(jnp.where(sel[0] == which, i, 0) for i in index(*ids))

    return pl.BlockSpec(shape, index_map)


def on_pick(sel, own, other, body):
    @pl.when(sel[0] == 0)
    def _():
        body(*own)

    @pl.when(sel[0] != 0)
    def _():
        body(*other)


def center(x):
    c = x - jnp.mean(x, axis=1, keepdims=True)
    r = lax.rsqrt(jnp.mean(c * c, axis=1, keepdims=True) + EPSILON)
    return c * r, r


def norm_first_kernel(x, gain, shift, o):
    n, _ = center(x[...].astype(F32))
    o[...] = (n * gain[...] + shift[...]).astype(BF)


def norm_first(x, gain, shift):
    return call(
        norm_first_kernel, (1,), (), (x, gain, shift),
        [whole(x.shape), whole(gain.shape), whole(shift.shape)],
        sds(x.shape, BF), whole(x.shape), 10 * x.size, "norm_first",
    )


def norm_next_kernel(x, branch, bias, gain, shift, y, o):
    total = x[...].astype(F32) + branch[...].astype(F32) + bias[...]
    rounded = total.astype(BF)
    y[...] = rounded
    n, _ = center(rounded.astype(F32))
    o[...] = (n * gain[...] + shift[...]).astype(BF)


def norm_next(x, branch, bias, gain, shift):
    v = whole(gain.shape)
    return call(
        norm_next_kernel, (1,), (), (x, branch, bias, gain, shift),
        [whole(x.shape), whole(x.shape), v, v, v],
        (sds(x.shape, BF), sds(x.shape, BF)), (whole(x.shape), whole(x.shape)),
        12 * x.size, "norm_next",
    )


def norm_back_kernel(x, gn, g, gain, gx, sums):
    n, r = center(x[...].astype(F32))
    up = gn[...].astype(F32)
    out = g[...].astype(F32)
    s = up * gain[...]
    gx[...] = (
        out
        + r * (s - jnp.mean(s, axis=1, keepdims=True) - n * jnp.mean(s * n, axis=1, keepdims=True))
    ).astype(BF)
    sums[0:1, :] = jnp.sum(up * n, axis=0, keepdims=True)
    sums[1:2, :] = jnp.sum(up, axis=0, keepdims=True)
    sums[2:3, :] = jnp.sum(out, axis=0, keepdims=True)


def norm_back(x, gn, g, gain):
    w = whole(x.shape)
    return call(
        norm_back_kernel, (1,), (), (x, gn, g, gain),
        [w, w, w, whole(gain.shape)],
        (sds(x.shape, BF), sds((3, x.shape[1]), F32)), (w, whole((3, x.shape[1]))),
        20 * x.size, "norm_back",
    )


def turn(a, cosine, low, high, sign):
    width = a.shape[-1]
    half = ROT // 2
    up = pltpu.roll(a, width - half, 1) * low
    down = pltpu.roll(a, half, 1) * high
    return a * cosine + (down - up if sign > 0 else up - down)


def project_kernel(sel, x, own, other, bias, cosine, low, high, q, kv):
    step = pl.program_id(0)

    def body(w):
        a = dot(x[...], w[0]) + bias[0]

        @pl.when(step == 0)
        def _():
            kv[0] = turn(a, cosine[...], low[...], high[...], 1).astype(BF)

        @pl.when(step == 1)
        def _():
            kv[0] = a.astype(BF)

        @pl.when(step == 2)
        def _():
            q[...] = turn(a, cosine[...], low[...], high[...], 1).astype(BF)

    on_pick(sel, (own,), (other,), body)


def project(sel, x, own, other, bias, tables):
    rows, width = x.shape
    local = own.shape[2]
    blk = min(256, local)
    n = local // blk

    def w_index(c, j):
        return (lax.rem(c + 1, 3), 0, j)

    table = whole((rows, blk))
    return call(
        project_kernel, (3, n), (sel,), (x, own, other, bias, *tables),
        [
            whole(x.shape),
            picked((1, width, blk), 0, w_index),
            picked((1, width, blk), 1, w_index),
            pl.BlockSpec((1, 1, blk), lambda c, j, s: (lax.rem(c + 1, 3), 0, j)),
            table, table, table,
        ],
        (sds((rows, local), BF), sds((2, rows, local), BF)),
        (
            pl.BlockSpec((rows, blk), lambda c, j, s: (0, jnp.where(c == 2, j, 0))),
            pl.BlockSpec(
                (1, rows, blk),
                lambda c, j, s: (jnp.minimum(c, 1), 0, jnp.where(c == 2, n - 1, j)),
            ),
        ),
        6 * rows * width * local, "project", moved=nbytes(own, x) + 6 * rows * local,
    )


def expand_kernel(sel, x, own, other, bias, gelu, slope):
    def body(w):
        u = dot(x[...], w[...]) + bias[...]
        t = jnp.tanh(GELU_ROOT * (u + GELU_CUBE * u * u * u))
        gelu[...] = (0.5 * u * (1.0 + t)).astype(BF)
        slope[...] = (
            0.5 * (1.0 + t)
            + 0.5 * u * (1.0 - t * t) * GELU_ROOT * (1.0 + 3.0 * GELU_CUBE * u * u)
        ).astype(BF)

    on_pick(sel, (own,), (other,), body)


def expand(sel, x, own, other, bias):
    rows, width = x.shape
    hidden = own.shape[1]
    blk = 256
    out = pl.BlockSpec((rows, blk), lambda j, s: (0, j))
    return call(
        expand_kernel, (hidden // blk,), (sel,), (x, own, other, bias),
        [
            whole(x.shape),
            picked((width, blk), 0, lambda j: (0, j)),
            picked((width, blk), 1, lambda j: (0, j)),
            pl.BlockSpec((1, blk), lambda j, s: (0, j)),
        ],
        (sds((rows, hidden), BF), sds((rows, hidden), BF)), (out, out),
        2 * rows * width * hidden, "expand", moved=nbytes(own, x) + 4 * rows * hidden,
    )


def contract_kernel(sel, a, u, d_own, f_own, d_other, f_other, o):
    def body(d, f):
        o[...] = (dot(a[...], d[...]) + dot(u[...], f[...])).astype(BF)

    on_pick(sel, (d_own, f_own), (d_other, f_other), body)


def contract(sel, a, u, d_own, f_own, d_other, f_other):
    rows, local = a.shape
    hidden = u.shape[1]
    width = d_own.shape[1]
    blk = 256
    specs = [
        picked((k, blk), which, lambda j: (0, j)) for which in (0, 1) for k in (local, hidden)
    ]
    return call(
        contract_kernel, (width // blk,), (sel,), (a, u, d_own, f_own, d_other, f_other),
        [whole(a.shape), whole(u.shape)] + specs,
        sds((rows, width), BF), pl.BlockSpec((rows, blk), lambda j, s: (0, j)),
        2 * rows * (local + hidden) * width, "contract",
        moved=nbytes(a, u, d_own, f_own) + 2 * rows * width,
    )


def masks_of(blocks, rows, drow, dcol):
    found = []
    for j in range(blocks):
        same = dcol[j * rows : (j + 1) * rows, :] == drow[...]
        if j == 0:
            key = lax.broadcasted_iota(jnp.int32, (rows, rows), 0)
            query = lax.broadcasted_iota(jnp.int32, (rows, rows), 1)
            same = same & (key <= query)
        found.append(same)
    return found


def attend_kernel(blocks, *refs):
    q, drow, dcol = refs[0], refs[1], refs[2]
    kvs = refs[3 : 3 + blocks]
    o, lse = refs[3 + blocks :]
    rows = q.shape[0]
    first = lax.broadcasted_iota(jnp.int32, (rows, PAIR), 1) < HEAD
    scaled = q[...] * HEAD ** (-0.5)
    allowed = masks_of(blocks, rows, drow, dcol)
    halves = []
    for h in range(2):
        qh = jnp.where(first if h == 0 else ~first, scaled, jnp.zeros_like(scaled))
        scores = [
            jnp.where(allowed[j], dot(kvs[j][0], qh, NT), NEGATIVE) for j in range(blocks)
        ]
        top = functools.reduce(
            jnp.maximum, [jnp.max(s, axis=0, keepdims=True) for s in scores]
        )
        weights = [jnp.exp(s - top) for s in scores]
        total = sum(jnp.sum(w, axis=0, keepdims=True) for w in weights)
        out = sum(dot(kvs[j][1], weights[j].astype(BF), TN) for j in range(blocks))
        halves.append((out / total)[h * HEAD : (h + 1) * HEAD])
        lse[0, h : h + 1, :] = top + jnp.log(total)
    o[...] = jnp.transpose(jnp.concatenate(halves, axis=0)).astype(BF)


def attend(q, kvs, drow, dcol):
    rows, local = q.shape
    blocks = len(kvs)
    pairs = local // PAIR
    return call(
        functools.partial(attend_kernel, blocks), (pairs,), (), (q, drow, dcol, *kvs),
        [
            pl.BlockSpec((rows, PAIR), lambda p: (0, p)),
            whole(drow.shape), whole(dcol.shape),
        ]
        + [pl.BlockSpec((2, rows, PAIR), lambda p: (0, 0, p))] * blocks,
        (sds((rows, local), BF), sds((pairs, 8, rows), F32)),
        (
            pl.BlockSpec((rows, PAIR), lambda p: (0, p)),
            pl.BlockSpec((1, 8, rows), lambda p: (p, 0, 0)),
        ),
        8 * rows * rows * blocks * local, "attend",
    )


def attend_back_kernel(blocks, *refs):
    q, go, lse, drow, dcol, cosine, low, high = refs[:8]
    kvs = refs[8 : 8 + blocks]
    gq = refs[8 + blocks]
    gkvs = refs[9 + blocks :]
    rows = q.shape[0]
    first = lax.broadcasted_iota(jnp.int32, (rows, PAIR), 1) < HEAD
    scaled = q[...] * HEAD ** (-0.5)
    gout = go[...]
    allowed = masks_of(blocks, rows, drow, dcol)
    gk = [0.0] * blocks
    gv = [0.0] * blocks
    halves = []
    for h in range(2):
        mine = first if h == 0 else ~first
        qh = jnp.where(mine, scaled, jnp.zeros_like(scaled))
        gh = jnp.where(mine, gout, jnp.zeros_like(gout))
        shift = lse[0, h : h + 1, :]
        probs = [
            jnp.where(allowed[j], jnp.exp(dot(kvs[j][0], qh, NT) - shift), 0.0)
            for j in range(blocks)
        ]
        gprobs = [dot(kvs[j][1], gh, NT) for j in range(blocks)]
        delta = sum(
            jnp.sum(probs[j] * gprobs[j], axis=0, keepdims=True) for j in range(blocks)
        )
        gqt = 0.0
        for j in range(blocks):
            gs = (probs[j] * (gprobs[j] - delta)).astype(BF)
            gk[j] += dot(gs, qh)
            gv[j] += dot(probs[j].astype(BF), gh)
            gqt += dot(kvs[j][0], gs, TN)
        halves.append(gqt[h * HEAD : (h + 1) * HEAD])
    full = jnp.transpose(jnp.concatenate(halves, axis=0)) * HEAD ** (-0.5)
    gq[...] = turn(full, cosine[...], low[...], high[...], -1).astype(BF)
    for j in range(blocks):
        gkvs[j][0] = gk[j].astype(gkvs[j].dtype)
        gkvs[j][1] = gv[j].astype(gkvs[j].dtype)


def attend_back(q, kvs, go, lse, drow, dcol, tables):
    rows, local = q.shape
    blocks = len(kvs)
    pair = pl.BlockSpec((rows, PAIR), lambda p: (0, p))
    two = pl.BlockSpec((2, rows, PAIR), lambda p: (0, 0, p))
    table = pl.BlockSpec((rows, PAIR), lambda p: (0, 0))
    return call(
        functools.partial(attend_back_kernel, blocks), (local // PAIR,), (),
        (q, go, lse, drow, dcol, *tables, *kvs),
        [
            pair, pair, pl.BlockSpec((1, 8, rows), lambda p: (p, 0, 0)),
            whole(drow.shape), whole(dcol.shape), table, table, table,
        ]
        + [two] * blocks,
        (sds((rows, local), BF),)
        + tuple(sds((2, rows, local), F32 if j == 0 else BF) for j in range(blocks)),
        (pair,) + (two,) * blocks,
        20 * rows * rows * blocks * local, "attend_back",
    )


def join_kernel(count, *refs):
    gq, own = refs[0], refs[1]
    got = refs[2 : 2 + count]
    cosine, low, high, out = refs[2 + count :]
    gk = sum((r[0].astype(F32) for r in got), own[0])
    gv = sum((r[1].astype(F32) for r in got), own[1])
    out[0] = gq[...]
    out[1] = turn(gk, cosine[...], low[...], high[...], -1).astype(BF)
    out[2] = gv.astype(BF)


def join(gq, own, got, tables):
    rows, local = gq.shape
    two = pl.BlockSpec((2, rows, PAIR), lambda p: (0, 0, p))
    table = pl.BlockSpec((rows, PAIR), lambda p: (0, 0))
    return call(
        functools.partial(join_kernel, len(got)), (local // PAIR,), (), (gq, own, *got, *tables),
        [pl.BlockSpec((rows, PAIR), lambda p: (0, p)), two] + [two] * len(got) + [table] * 3,
        sds((3, rows, local), BF), pl.BlockSpec((3, rows, PAIR), lambda p: (0, 0, p)),
        10 * own.size, "join",
    )


def spread_attn_kernel(sel, g, own, other, o):
    def body(w):
        o[...] = dot(g[...], w[...], NT).astype(BF)

    on_pick(sel, (own,), (other,), body)


def spread_attn(sel, g, own, other):
    rows, width = g.shape
    local = own.shape[0]
    blk = min(256, local)
    return call(
        spread_attn_kernel, (local // blk,), (sel,), (g, own, other),
        [
            whole(g.shape),
            picked((blk, width), 0, lambda j: (j, 0)),
            picked((blk, width), 1, lambda j: (j, 0)),
        ],
        sds((rows, local), BF), pl.BlockSpec((rows, blk), lambda j, s: (0, j)),
        2 * rows * width * local, "spread_attn", moved=nbytes(g, own) + 2 * rows * local,
    )


def spread_up_kernel(sel, g, own, other, slope, o, sums):
    def body(w):
        u = (dot(g[...], w[...], NT) * slope[...].astype(F32)).astype(BF)
        o[...] = u
        sums[...] = jnp.sum(u.astype(F32), axis=0, keepdims=True)

    on_pick(sel, (own,), (other,), body)


def spread_up(sel, g, own, other, slope):
    rows, width = g.shape
    hidden = own.shape[0]
    blk = 256
    col = pl.BlockSpec((rows, blk), lambda j, s: (0, j))
    return call(
        spread_up_kernel, (hidden // blk,), (sel,), (g, own, other, slope),
        [
            whole(g.shape),
            picked((blk, width), 0, lambda j: (j, 0)),
            picked((blk, width), 1, lambda j: (j, 0)),
            col,
        ],
        (sds((rows, hidden), BF), sds((1, hidden), F32)),
        (col, pl.BlockSpec((1, blk), lambda j, s: (0, j))),
        2 * rows * width * hidden, "spread_up", moved=nbytes(g, own, slope) + 2 * rows * hidden,
    )


def gather_grad_kernel(sel, qkv, up, w_own, f_own, w_other, f_other, o, sums):
    def body(w, f):
        a = dot(up[...], f[...], NT)
        for c in range(3):
            a += dot(qkv[c], w[c], NT)
        o[...] = a.astype(BF)

    on_pick(sel, (w_own, f_own), (w_other, f_other), body)

    @pl.when(pl.program_id(0) == 0)
    def _():
        for c in range(3):
            sums[c : c + 1, :] = jnp.sum(qkv[c].astype(F32), axis=0, keepdims=True)


def gather_grad(sel, qkv, up, w_own, f_own, w_other, f_other):
    _, rows, local = qkv.shape
    hidden = up.shape[1]
    width = f_own.shape[0]
    blk = 256
    specs = []
    for which in (0, 1):
        specs.append(picked((3, blk, local), which, lambda j: (0, j, 0)))
        specs.append(picked((blk, hidden), which, lambda j: (j, 0)))
    return call(
        gather_grad_kernel, (width // blk,), (sel,), (qkv, up, w_own, f_own, w_other, f_other),
        [whole(qkv.shape), whole(up.shape)] + specs,
        (sds((rows, width), BF), sds((3, local), F32)),
        (pl.BlockSpec((rows, blk), lambda j, s: (0, j)), whole((3, local))),
        2 * rows * width * (3 * local + hidden), "gather_grad",
        moved=nbytes(qkv, up, w_own, f_own) + 2 * rows * width,
    )


def weight_kernel(count, adds, half, *refs):
    lhs, rhs = refs[:count], refs[count : 2 * count]
    a = sum(dot(x[...], y[0], TN) for x, y in zip(lhs, rhs))
    if adds:
        a += refs[2 * count][0].astype(F32)
    refs[-1][0] = a.astype(BF)


def weight_half(half, lhs, rhs, add=None):
    rows, depth = lhs[0].shape
    planes, _, cols = rhs[0].shape
    blk = min(256, depth // 2)
    n = depth // 2 // blk
    ins = (*lhs, *rhs) + (() if add is None else (add,))
    out = pl.BlockSpec((1, blk, cols), lambda c, i, h: (c, i, 0))
    return call(
        functools.partial(weight_kernel, len(lhs), add is not None), (planes, n), (half,), ins,
        [pl.BlockSpec((rows, blk), lambda c, i, h: (0, h[0] * n + i))] * len(lhs)
        + [pl.BlockSpec((1, rows, cols), lambda c, i, h: (c, 0, 0))] * len(rhs)
        + ([] if add is None else [out]),
        sds((planes, depth // 2, cols), BF), out,
        len(lhs) * rows * depth * cols * planes, "weight_half",
    )


def widen_kernel(sec, own0, own1, got0, got1, o):
    half = pl.program_id(1)
    mine = half == sec[0]
    for layer, own, got in ((0, own0, got0), (1, own1, got1)):
        here = sec[0] == layer

        @pl.when(here & mine)
        def _():
            o[...] = own[...].astype(F32)

        @pl.when(here & ~mine)
        def _():
            o[...] = got[...].astype(F32)


def widen(sec, own, got):
    planes, depth, cols = own[0].shape
    blk = min(256, depth)
    n = depth // blk

    def spec(layer, from_own):
        def index_map(c, h, i, s):
            use = (s[0] == layer) & ((h == s[0]) == from_own)
            return (jnp.where(use, c, 0), jnp.where(use, i, 0), 0)

        return pl.BlockSpec((1, blk, cols), index_map)

    return call(
        widen_kernel, (planes, 2, n), (sec,), (*own, *got),
        [spec(0, True), spec(1, True), spec(0, False), spec(1, False)],
        sds((planes, 2 * depth, cols), F32),
        pl.BlockSpec((1, blk, cols), lambda c, h, i, s: (c, h * n + i, 0)),
        own[0].size, "widen", moved=12 * own[0].size,
    )


def swap_sections(x):
    return lax.ppermute(x, "section", [(0, 1), (1, 0)])


def shift_ctx(x, by):
    length = lax.axis_size("ctx")
    return lax.ppermute(
        x, "ctx", [(i, i + by) for i in range(length) if 0 <= i + by < length]
    )


def rope_tables(positions, width):
    half = ROT // 2
    frequency = 10000.0 ** (-(2.0 * jnp.arange(half, dtype=F32)) / ROT)
    angles = positions.astype(F32)[:, None] * frequency[None, :]
    c, s = jnp.cos(angles), jnp.sin(angles)
    zero = jnp.zeros_like(c)
    one = jnp.ones_like(c)

    def lay(*parts):
        head = jnp.concatenate(parts, axis=1)
        return jnp.tile(head, (1, width // HEAD))

    return lay(c, c, one, one), lay(s, zero, zero, zero), lay(zero, s, zero, zero)


def on_device(
    inputs,
    segments,
    cotangent,
    ln_gain,
    ln_bias,
    qkv_weight,
    qkv_bias,
    dense_weight,
    fc1_weight,
    fc1_bias,
    fc2_weight,
    out_bias,
):
    sections = lax.axis_size("section")
    section = lax.axis_index("section")
    ctx_id = lax.axis_index("ctx")
    ctx = lax.axis_size("ctx")
    batches, r, width = inputs.shape
    rows = r * lax.axis_size("tp")
    total_rows = rows * ctx
    local = qkv_weight.shape[3]
    hidden = fc1_weight.shape[2]
    mine = batches // sections
    back = (total_rows // 2) // rows
    blocks = min(back, ctx - 1) + 1
    first_mb = section * mine
    layers = (0, 1)

    small = jnp.concatenate(
        [ln_gain[0], ln_bias[0], out_bias[0], qkv_bias[0].reshape(-1), fc1_bias[0]]
    )
    small_other = swap_sections(small)
    w_own = (qkv_weight[0], fc1_weight[0], dense_weight[0], fc2_weight[0])
    w_other = tuple(swap_sections(w) for w in w_own)
    sel, gain, shift, obias, qkv_b, fc1_b = [], [], [], [], [], []
    for layer in layers:
        sel.append((section != layer).astype(jnp.int32).reshape(1))
        v = jnp.where(section == layer, small, small_other).astype(F32)
        gain.append(v[:width].reshape(1, width))
        shift.append(v[width : 2 * width].reshape(1, width))
        obias.append(v[2 * width : 3 * width].reshape(1, width))
        qkv_b.append(v[3 * width : 3 * width + 3 * local].reshape(3, 1, local))
        fc1_b.append(v[3 * width + 3 * local :].reshape(1, hidden))

    positions = ctx_id * rows + jnp.arange(rows, dtype=jnp.int32)
    wide = rope_tables(positions, min(256, local))
    tables = tuple(t[:, :PAIR] for t in wide)

    docs = lax.dynamic_slice_in_dim(segments, first_mb, mine, 0)
    padded = jnp.pad(docs, ((0, 0), ((blocks - 1) * rows, 0)), constant_values=-1)
    window = lax.dynamic_slice_in_dim(padded, ctx_id * rows, blocks * rows, 1)
    window = window.reshape(mine, blocks, rows)[:, ::-1]
    drow = [window[m, 0].reshape(1, rows) for m in range(mine)]
    dcol = [window[m].reshape(blocks * rows, 1) for m in range(mine)]

    x_in = lax.dynamic_slice_in_dim(inputs, first_mb, mine, 0)
    g_in = lax.dynamic_slice_in_dim(cotangent, first_mb, mine, 0)

    def gather(v):
        return lax.all_gather(v, "tp", axis=0, tiled=True)

    def scatter(v):
        return lax.psum_scatter(v, "tp", scatter_dimension=0, tiled=True)

    qw, fw, dw, ow = zip(w_own, w_other)
    kept = {}
    x = [x_in[m] for m in range(mine)]
    normed = [norm_first(x[m], gain[0], shift[0]) for m in range(mine)]
    outs = []
    for layer in layers:
        branch = []
        for m in range(mine):
            full = gather(normed[m])
            q, kv = project(sel[layer], full, *qw, qkv_b[layer], wide)
            kvs = [kv] + [shift_ctx(kv, j) for j in range(1, blocks)]
            gelu, slope = expand(sel[layer], full, *fw, fc1_b[layer])
            attended, lse = attend(q, kvs, drow[m], dcol[m])
            branch.append(
                scatter(contract(sel[layer], attended, gelu, dw[0], ow[0], dw[1], ow[1]))
            )
            kept[layer, m] = (x[m], full, q, kvs, gelu, slope, attended, lse)
        if layer + 1 < len(layers):
            pairs = [
                norm_next(x[m], branch[m], obias[layer], gain[layer + 1], shift[layer + 1])
                for m in range(mine)
            ]
            x = [p[0] for p in pairs]
            normed = [p[1] for p in pairs]
            outs.append(jnp.stack(x))
        else:
            outs.append(
                jnp.stack(
                    [
                        (x[m].astype(F32) + branch[m].astype(F32) + obias[layer]).astype(BF)
                        for m in range(mine)
                    ]
                )
            )

    g = [g_in[m] for m in range(mine)]
    gin = {}
    sums = {}
    biases = {}
    halves = {}
    keep_half = section.astype(jnp.int32).reshape(1)
    send_half = 1 - keep_half
    for layer in reversed(layers):
        gfull = [gather(g[m]) for m in range(mine)]
        up, qkv_g, gx = [], [], []
        rowsum, bq, bu = 0.0, 0.0, 0.0
        for m in range(mine):
            x_l, full, q, kvs, gelu, slope, attended, lse = kept[layer, m]
            ga = spread_attn(sel[layer], gfull[m], *dw)
            back_out = attend_back(q, kvs, ga, lse, drow[m], dcol[m], tables)
            got = [shift_ctx(back_out[1 + j], -j) for j in range(1, blocks)]
            u, usum = spread_up(sel[layer], gfull[m], *ow, slope)
            p = join(back_out[0], back_out[1], got, tables)
            partial, qsum = gather_grad(sel[layer], p, u, qw[0], fw[0], qw[1], fw[1])
            gx_m, s = norm_back(x_l, scatter(partial), g[m], gain[layer])
            up.append(u)
            qkv_g.append(p)
            gx.append(gx_m)
            rowsum, bq, bu = rowsum + s, bq + qsum, bu + usum
        sums[layer] = rowsum
        biases[layer] = jnp.concatenate([bq.reshape(-1), bu.reshape(-1)])
        fulls = [kept[layer, m][1] for m in range(mine)]
        attn = [kept[layer, m][6] for m in range(mine)]
        gelus = [kept[layer, m][4] for m in range(mine)]
        gplane = [v[None] for v in gfull]
        uplane = [v[None] for v in up]
        jobs = ((attn, gplane), (gelus, gplane), (fulls, uplane), (fulls, qkv_g))
        reduced = []
        for lhs, rhs in jobs:
            got = swap_sections(weight_half(send_half, lhs, rhs))
            reduced.append(lax.psum(weight_half(keep_half, lhs, rhs, got), "ctx"))
        halves[layer] = reduced
        g = gx
        gin[layer] = jnp.stack(gx)

    def to_owner(pair_of):
        moved = swap_sections(jnp.where(section == 0, pair_of[1], pair_of[0]))
        own = jnp.where(section == 0, pair_of[0], pair_of[1])
        return jnp.where(
            section == 0,
            jnp.concatenate([own, moved], axis=0),
            jnp.concatenate([moved, own], axis=0),
        )

    layer_out = to_owner(outs)
    grad_in = to_owner([gin[0], gin[1]])

    final = []
    for k in range(4):
        own = [halves[layer][k] for layer in layers]
        got = [
            lax.ppermute(own[layer], "section", [(1 - layer, layer)]) for layer in layers
        ]
        final.append(widen(keep_half, own, got))
    dense_g, fc2_g, fc1_g, qkv_gr = final

    rowsum = lax.psum(jnp.stack([sums[0], sums[1]]), ("section", "ctx", "tp"))
    rowsum = jnp.where(section == 0, rowsum[0], rowsum[1])
    bias_sum = lax.psum(jnp.stack([biases[0], biases[1]]), ("section", "ctx"))
    bias_sum = jnp.where(section == 0, bias_sum[0], bias_sum[1])

    return (
        layer_out[None],
        grad_in[None],
        rowsum[0][None],
        rowsum[1][None],
        qkv_gr[None],
        bias_sum[: 3 * local].reshape(3, local)[None],
        dense_g,
        fc1_g,
        bias_sum[3 * local :][None],
        fc2_g,
        rowsum[2][None],
    )


def solution(mesh):
    return jax.shard_map(
        on_device,
        mesh=mesh,
        in_specs=(
            P(None, ("ctx", "tp"), None),
            P(),
            P(None, ("ctx", "tp"), None),
            P("section", None),
            P("section", None),
            P("section", None, None, "tp"),
            P("section", None, "tp"),
            P("section", "tp", None),
            P("section", None, "tp"),
            P("section", "tp"),
            P("section", "tp", None),
            P("section", None),
        ),
        out_specs=(
            P("section", None, ("ctx", "tp"), None),
            P("section", None, ("ctx", "tp"), None),
            P("section", None),
            P("section", None),
            P("section", None, None, "tp"),
            P("section", None, "tp"),
            P("section", "tp", None),
            P("section", None, "tp"),
            P("section", "tp"),
            P("section", "tp", None),
            P("section", None),
        ),
        check_vma=False,
    )
```

```python
import functools

import jax
import jax.numpy as jnp
from jax import lax
from jax.experimental import pallas as pl
from jax.experimental.pallas import tpu as pltpu
from jax.sharding import PartitionSpec as P

HEAD = 64
ROT = 32
PAIR = 2 * HEAD

EPSILON = 1e-05
NEGATIVE = -1e30
GELU_ROOT = 0.7978845608028654
GELU_CUBE = 0.044715

BF = jnp.bfloat16
F32 = jnp.float32
NT = (((1,), (1,)), ((), ()))
TN = (((0,), (0,)), ((), ()))
VMEM_LIMIT = 60 * 1024 * 1024


def sds(shape, dtype):
    return jax.ShapeDtypeStruct(shape, dtype)


def nbytes(*arrays):
    return sum(a.size * a.dtype.itemsize for a in arrays)


def call(kernel, grid, scalars, ins, in_specs, outs, out_specs, flops, name, scratch=(), moved=None):
    return pl.pallas_call(
        kernel,
        grid_spec=pltpu.PrefetchScalarGridSpec(
            num_scalar_prefetch=len(scalars),
            grid=grid,
            in_specs=in_specs,
            out_specs=out_specs,
            scratch_shapes=scratch,
        ),
        out_shape=outs,
        name=name,
        cost_estimate=pl.CostEstimate(
            flops=int(flops),
            bytes_accessed=int(moved if moved is not None else nbytes(*ins) + nbytes(*jax.tree.leaves(outs))),
            transcendentals=0,
        ),
        compiler_params=pltpu.CompilerParams(vmem_limit_bytes=VMEM_LIMIT),
    )(*scalars, *ins)


def dot(a, b, dims=(((1,), (0,)), ((), ()))):
    return lax.dot_general(a, b, dims, preferred_element_type=F32)


def whole(shape):
    return pl.BlockSpec(shape, lambda *_: (0,) * len(shape))


def stream(name, sel, xs, weights, n, extra, extra_specs, outs, out_specs, body, flops):
    nx, nw, ne, no = len(xs), len(weights), len(extra), len(outs)

    def kernel(*refs):
        pick_ref, refs = refs[0], refs[1:]
        x_refs, refs = refs[:nx], refs[nx:]
        own, refs = refs[:nw], refs[nw:]
        other, refs = refs[:nw], refs[nw:]
        extra_refs, refs = refs[:ne], refs[ne:]
        out_refs, refs = refs[:no], refs[no:]
        x_buf, refs = refs[:nx], refs[nx:]
        w_buf, (x_sem, w_sem) = refs[:nw], refs[nw:]
        j = pl.program_id(0)

        def weight_copy(side, k, i):
            return pltpu.make_async_copy(
                weights[k][3](side[k], i), w_buf[k].at[i], w_sem.at[k, i]
            )

        @pl.when(j == 0)
        def _():
            copies = [
                pltpu.make_async_copy(x_refs[i], x_buf[i], x_sem.at[i]) for i in range(nx)
            ]
            for c in copies:
                c.start()

            @pl.when(pick_ref[0] == 0)
            def _():
                for i in range(n):
                    for k in range(nw):
                        weight_copy(own, k, i).start()

            @pl.when(pick_ref[0] != 0)
            def _():
                for i in range(n):
                    for k in range(nw):
                        weight_copy(other, k, i).start()

            for c in copies:
                c.wait()

        for k in range(nw):
            weight_copy(own, k, j).wait()
        body(j, x_buf, [w_buf[k].at[j] for k in range(nw)], extra_refs, out_refs)

    own = [w[0] for w in weights]
    other = [w[1] for w in weights]
    hbm = pl.BlockSpec(memory_space=pl.ANY)
    scratch = [pltpu.VMEM(x.shape, x.dtype) for x in xs]
    scratch += [pltpu.VMEM((n,) + tuple(w[2]), BF) for w in weights]
    scratch += [pltpu.SemaphoreType.DMA((nx,)), pltpu.SemaphoreType.DMA((nw, n))]
    return call(
        kernel, (n,), (sel,), (*xs, *own, *other, *extra),
        [hbm] * (nx + 2 * nw) + list(extra_specs), outs, out_specs, flops, name,
        scratch=scratch, moved=nbytes(*xs, *own, *extra) + nbytes(*outs),
    )


def center(x):
    c = x - jnp.mean(x, axis=1, keepdims=True)
    r = lax.rsqrt(jnp.mean(c * c, axis=1, keepdims=True) + EPSILON)
    return c * r, r


def norm_first_kernel(x, gain, shift, o):
    n, _ = center(x[...].astype(F32))
    o[...] = (n * gain[...] + shift[...]).astype(BF)


def norm_first(x, gain, shift):
    return call(
        norm_first_kernel, (1,), (), (x, gain, shift),
        [whole(x.shape), whole(gain.shape), whole(shift.shape)],
        sds(x.shape, BF), whole(x.shape), 10 * x.size, "norm_first",
    )


def norm_next_kernel(x, branch, bias, gain, shift, y, o):
    total = x[...].astype(F32) + branch[...].astype(F32) + bias[...]
    rounded = total.astype(BF)
    y[...] = rounded
    n, _ = center(rounded.astype(F32))
    o[...] = (n * gain[...] + shift[...]).astype(BF)


def norm_next(x, branch, bias, gain, shift):
    v = whole(gain.shape)
    return call(
        norm_next_kernel, (1,), (), (x, branch, bias, gain, shift),
        [whole(x.shape), whole(x.shape), v, v, v],
        (sds(x.shape, BF), sds(x.shape, BF)), (whole(x.shape), whole(x.shape)),
        12 * x.size, "norm_next",
    )


def norm_back_kernel(x, gn, g, gain, gx, sums):
    n, r = center(x[...].astype(F32))
    up = gn[...].astype(F32)
    out = g[...].astype(F32)
    s = up * gain[...]
    gx[...] = (
        out
        + r * (s - jnp.mean(s, axis=1, keepdims=True) - n * jnp.mean(s * n, axis=1, keepdims=True))
    ).astype(BF)
    sums[0:1, :] = jnp.sum(up * n, axis=0, keepdims=True)
    sums[1:2, :] = jnp.sum(up, axis=0, keepdims=True)
    sums[2:3, :] = jnp.sum(out, axis=0, keepdims=True)


def norm_back(x, gn, g, gain):
    w = whole(x.shape)
    return call(
        norm_back_kernel, (1,), (), (x, gn, g, gain),
        [w, w, w, whole(gain.shape)],
        (sds(x.shape, BF), sds((3, x.shape[1]), F32)), (w, whole((3, x.shape[1]))),
        20 * x.size, "norm_back",
    )


def turn(a, cosine, low, high, sign):
    width = a.shape[-1]
    half = ROT // 2
    up = pltpu.roll(a, width - half, 1) * low
    down = pltpu.roll(a, half, 1) * high
    return a * cosine + (down - up if sign > 0 else up - down)


def project(sel, x, own, other, bias, tables):
    rows, width = x.shape
    local = own.shape[2]

    def body(j, xs, ws, extra, out):
        bias_ref, cosine, low, high = extra
        q, kv = out
        a = dot(xs[0][...], ws[0][...]) + bias_ref[0]

        def turned(to):
            for p in range(0, local, PAIR):
                piece = turn(a[:, p : p + PAIR], cosine[...], low[...], high[...], 1)
                to[:, p : p + PAIR] = piece.astype(BF)

        @pl.when(j == 0)
        def _():
            turned(kv.at[0])

        @pl.when(j == 1)
        def _():
            kv[0] = a.astype(BF)

        @pl.when(j == 2)
        def _():
            turned(q)

    table = whole((rows, PAIR))
    return stream(
        "project", sel, [x],
        [(own, other, (width, local), lambda w, i: w.at[lax.rem(i + 1, 3)])], 3,
        (bias, *tables),
        [pl.BlockSpec((1, 1, local), lambda j, s: (lax.rem(j + 1, 3), 0, 0))] + [table] * 3,
        (sds((rows, local), BF), sds((2, rows, local), BF)),
        (
            whole((rows, local)),
            pl.BlockSpec((1, rows, local), lambda j, s: (jnp.minimum(j, 1), 0, 0)),
        ),
        body, 6 * rows * width * local,
    )


def columns(blk):
    return lambda w, i: w.at[:, pl.ds(pl.multiple_of(i * blk, blk), blk)]


def lines(blk):
    return lambda w, i: w.at[pl.ds(pl.multiple_of(i * blk, blk), blk)]


def expand(sel, x, own, other, bias):
    rows, width = x.shape
    hidden = own.shape[1]
    blk = 512

    def body(j, xs, ws, extra, out):
        u = dot(xs[0][...], ws[0][...]) + extra[0][...]
        t = jnp.tanh(GELU_ROOT * (u + GELU_CUBE * u * u * u))
        out[0][...] = (0.5 * u * (1.0 + t)).astype(BF)
        out[1][...] = (
            0.5 * (1.0 + t)
            + 0.5 * u * (1.0 - t * t) * GELU_ROOT * (1.0 + 3.0 * GELU_CUBE * u * u)
        ).astype(BF)

    spec = pl.BlockSpec((rows, blk), lambda j, s: (0, j))
    return stream(
        "expand", sel, [x], [(own, other, (width, blk), columns(blk))], hidden // blk,
        (bias,), [pl.BlockSpec((1, blk), lambda j, s: (0, j))],
        (sds((rows, hidden), BF), sds((rows, hidden), BF)), (spec, spec),
        body, 2 * rows * width * hidden,
    )


def contract(sel, a, u, d_own, f_own, d_other, f_other):
    rows, local = a.shape
    hidden = u.shape[1]
    width = d_own.shape[1]
    blk = 512

    def body(j, xs, ws, extra, out):
        out[0][...] = (dot(xs[0][...], ws[0][...]) + dot(xs[1][...], ws[1][...])).astype(BF)

    return stream(
        "contract", sel, [a, u],
        [
            (d_own, d_other, (local, blk), columns(blk)),
            (f_own, f_other, (hidden, blk), columns(blk)),
        ],
        width // blk, (), [],
        (sds((rows, width), BF),), (pl.BlockSpec((rows, blk), lambda j, s: (0, j)),),
        body, 2 * rows * (local + hidden) * width,
    )[0]


def masks_of(blocks, rows, drow, dcol):
    found = []
    for j in range(blocks):
        same = dcol[j * rows : (j + 1) * rows, :] == drow[...]
        if j == 0:
            key = lax.broadcasted_iota(jnp.int32, (rows, rows), 0)
            query = lax.broadcasted_iota(jnp.int32, (rows, rows), 1)
            same = same & (key <= query)
        found.append(same)
    return found


def attend_kernel(blocks, *refs):
    q, drow, dcol = refs[0], refs[1], refs[2]
    kvs = refs[3 : 3 + blocks]
    o, lse = refs[3 + blocks :]
    rows = q.shape[0]
    first = lax.broadcasted_iota(jnp.int32, (rows, PAIR), 1) < HEAD
    scaled = q[...] * HEAD ** (-0.5)
    allowed = masks_of(blocks, rows, drow, dcol)
    halves = []
    for h in range(2):
        qh = jnp.where(first if h == 0 else ~first, scaled, jnp.zeros_like(scaled))
        scores = [
            jnp.where(allowed[j], dot(kvs[j][0], qh, NT), NEGATIVE) for j in range(blocks)
        ]
        top = functools.reduce(
            jnp.maximum, [jnp.max(s, axis=0, keepdims=True) for s in scores]
        )
        weights = [jnp.exp(s - top) for s in scores]
        total = sum(jnp.sum(w, axis=0, keepdims=True) for w in weights)
        out = sum(dot(kvs[j][1], weights[j].astype(BF), TN) for j in range(blocks))
        halves.append((out / total)[h * HEAD : (h + 1) * HEAD])
        lse[0, h : h + 1, :] = top + jnp.log(total)
    o[...] = jnp.transpose(jnp.concatenate(halves, axis=0)).astype(BF)


def attend(q, kvs, drow, dcol):
    rows, local = q.shape
    blocks = len(kvs)
    pairs = local // PAIR
    return call(
        functools.partial(attend_kernel, blocks), (pairs,), (), (q, drow, dcol, *kvs),
        [
            pl.BlockSpec((rows, PAIR), lambda p: (0, p)),
            whole(drow.shape), whole(dcol.shape),
        ]
        + [pl.BlockSpec((2, rows, PAIR), lambda p: (0, 0, p))] * blocks,
        (sds((rows, local), BF), sds((pairs, 8, rows), F32)),
        (
            pl.BlockSpec((rows, PAIR), lambda p: (0, p)),
            pl.BlockSpec((1, 8, rows), lambda p: (p, 0, 0)),
        ),
        8 * rows * rows * blocks * local, "attend",
    )


def attend_back_kernel(blocks, *refs):
    q, go, lse, drow, dcol, cosine, low, high = refs[:8]
    kvs = refs[8 : 8 + blocks]
    gq = refs[8 + blocks]
    gkvs = refs[9 + blocks :]
    rows = q.shape[0]
    first = lax.broadcasted_iota(jnp.int32, (rows, PAIR), 1) < HEAD
    scaled = q[...] * HEAD ** (-0.5)
    gout = go[...]
    allowed = masks_of(blocks, rows, drow, dcol)
    gk = [0.0] * blocks
    gv = [0.0] * blocks
    halves = []
    for h in range(2):
        mine = first if h == 0 else ~first
        qh = jnp.where(mine, scaled, jnp.zeros_like(scaled))
        gh = jnp.where(mine, gout, jnp.zeros_like(gout))
        shift = lse[0, h : h + 1, :]
        probs = [
            jnp.where(allowed[j], jnp.exp(dot(kvs[j][0], qh, NT) - shift), 0.0)
            for j in range(blocks)
        ]
        gprobs = [dot(kvs[j][1], gh, NT) for j in range(blocks)]
        delta = sum(
            jnp.sum(probs[j] * gprobs[j], axis=0, keepdims=True) for j in range(blocks)
        )
        gqt = 0.0
        for j in range(blocks):
            gs = (probs[j] * (gprobs[j] - delta)).astype(BF)
            gk[j] += dot(gs, qh)
            gv[j] += dot(probs[j].astype(BF), gh)
            gqt += dot(kvs[j][0], gs, TN)
        halves.append(gqt[h * HEAD : (h + 1) * HEAD])
    full = jnp.transpose(jnp.concatenate(halves, axis=0)) * HEAD ** (-0.5)
    gq[...] = turn(full, cosine[...], low[...], high[...], -1).astype(BF)
    for j in range(blocks):
        gkvs[j][0] = gk[j].astype(gkvs[j].dtype)
        gkvs[j][1] = gv[j].astype(gkvs[j].dtype)


def attend_back(q, kvs, go, lse, drow, dcol, tables):
    rows, local = q.shape
    blocks = len(kvs)
    pair = pl.BlockSpec((rows, PAIR), lambda p: (0, p))
    two = pl.BlockSpec((2, rows, PAIR), lambda p: (0, 0, p))
    table = pl.BlockSpec((rows, PAIR), lambda p: (0, 0))
    return call(
        functools.partial(attend_back_kernel, blocks), (local // PAIR,), (),
        (q, go, lse, drow, dcol, *tables, *kvs),
        [
            pair, pair, pl.BlockSpec((1, 8, rows), lambda p: (p, 0, 0)),
            whole(drow.shape), whole(dcol.shape), table, table, table,
        ]
        + [two] * blocks,
        (sds((rows, local), BF),)
        + tuple(sds((2, rows, local), F32 if j == 0 else BF) for j in range(blocks)),
        (pair,) + (two,) * blocks,
        20 * rows * rows * blocks * local, "attend_back",
    )


def join_kernel(count, *refs):
    gq, own = refs[0], refs[1]
    got = refs[2 : 2 + count]
    cosine, low, high, out = refs[2 + count :]
    out[0] = gq[...]
    out[2] = sum((r[1].astype(F32) for r in got), own[1]).astype(BF)
    for p in range(0, gq.shape[1], PAIR):
        at = slice(p, p + PAIR)
        gk = sum((r[0, :, at].astype(F32) for r in got), own[0, :, at])
        out[1, :, at] = turn(gk, cosine[...], low[...], high[...], -1).astype(BF)


def join(gq, own, got, tables):
    rows, local = gq.shape
    return call(
        functools.partial(join_kernel, len(got)), (1,), (), (gq, own, *got, *tables),
        [whole(gq.shape), whole(own.shape)]
        + [whole(own.shape)] * len(got)
        + [whole((rows, PAIR))] * 3,
        sds((3, rows, local), BF), whole((3, rows, local)), 10 * own.size, "join",
    )


def spread_attn(sel, g, own, other):
    rows, width = g.shape
    local = own.shape[0]
    blk = min(256, local)

    def body(j, xs, ws, extra, out):
        out[0][...] = dot(xs[0][...], ws[0][...], NT).astype(BF)

    return stream(
        "spread_attn", sel, [g], [(own, other, (blk, width), lines(blk))], local // blk,
        (), [], (sds((rows, local), BF),),
        (pl.BlockSpec((rows, blk), lambda j, s: (0, j)),), body, 2 * rows * width * local,
    )[0]


def spread_up(sel, g, own, other, slope):
    rows, width = g.shape
    hidden = own.shape[0]
    blk = 512

    def body(j, xs, ws, extra, out):
        u = (dot(xs[0][...], ws[0][...], NT) * extra[0][...].astype(F32)).astype(BF)
        out[0][...] = u
        out[1][...] = jnp.sum(u.astype(F32), axis=0, keepdims=True)

    col = pl.BlockSpec((rows, blk), lambda j, s: (0, j))
    return stream(
        "spread_up", sel, [g], [(own, other, (blk, width), lines(blk))], hidden // blk,
        (slope,), [col], (sds((rows, hidden), BF), sds((1, hidden), F32)),
        (col, pl.BlockSpec((1, blk), lambda j, s: (0, j))), body, 2 * rows * width * hidden,
    )


def gather_grad(sel, qkv, up, w_own, f_own, w_other, f_other):
    _, rows, local = qkv.shape
    hidden = up.shape[1]
    width = f_own.shape[0]
    blk = 512

    def body(j, xs, ws, extra, out):
        a = dot(xs[1][...], ws[1][...], NT)
        for c in range(3):
            a += dot(xs[0][c], ws[0][c], NT)
        out[0][...] = a.astype(BF)

        @pl.when(j == 0)
        def _():
            for c in range(3):
                out[1][c : c + 1, :] = jnp.sum(xs[0][c].astype(F32), axis=0, keepdims=True)

    return stream(
        "gather_grad", sel, [qkv, up],
        [
            (
                w_own, w_other, (3, blk, local),
                lambda w, i: w.at[:, pl.ds(pl.multiple_of(i * blk, blk), blk)],
            ),
            (f_own, f_other, (blk, hidden), lines(blk)),
        ],
        width // blk, (), [],
        (sds((rows, width), BF), sds((3, local), F32)),
        (pl.BlockSpec((rows, blk), lambda j, s: (0, j)), whole((3, local))),
        body, 2 * rows * width * (3 * local + hidden),
    )


def weight_kernel(count, adds, half, *refs):
    lhs, rhs = refs[:count], refs[count : 2 * count]
    a = sum(dot(x[...], y[0], TN) for x, y in zip(lhs, rhs))
    if adds:
        a += refs[2 * count][0].astype(F32)
    refs[-1][0] = a.astype(BF)


def weight_half(half, lhs, rhs, add=None):
    rows, depth = lhs[0].shape
    planes, _, cols = rhs[0].shape
    blk = min(256, depth // 2)
    n = depth // 2 // blk
    ins = (*lhs, *rhs) + (() if add is None else (add,))
    out = pl.BlockSpec((1, blk, cols), lambda c, i, h: (c, i, 0))
    return call(
        functools.partial(weight_kernel, len(lhs), add is not None), (planes, n), (half,), ins,
        [pl.BlockSpec((rows, blk), lambda c, i, h: (0, h[0] * n + i))] * len(lhs)
        + [pl.BlockSpec((1, rows, cols), lambda c, i, h: (c, 0, 0))] * len(rhs)
        + ([] if add is None else [out]),
        sds((planes, depth // 2, cols), BF), out,
        len(lhs) * rows * depth * cols * planes, "weight_half",
    )


def widen_kernel(sec, own0, own1, got0, got1, o):
    half = pl.program_id(1)
    mine = half == sec[0]
    for layer, own, got in ((0, own0, got0), (1, own1, got1)):
        here = sec[0] == layer

        @pl.when(here & mine)
        def _():
            o[...] = own[...].astype(F32)

        @pl.when(here & ~mine)
        def _():
            o[...] = got[...].astype(F32)


def widen(sec, own, got):
    planes, depth, cols = own[0].shape
    blk = min(256, depth)
    n = depth // blk

    def spec(layer, from_own):
        def index_map(c, h, i, s):
            use = (s[0] == layer) & ((h == s[0]) == from_own)
            return (jnp.where(use, c, 0), jnp.where(use, i, 0), 0)

        return pl.BlockSpec((1, blk, cols), index_map)

    return call(
        widen_kernel, (planes, 2, n), (sec,), (*own, *got),
        [spec(0, True), spec(1, True), spec(0, False), spec(1, False)],
        sds((planes, 2 * depth, cols), F32),
        pl.BlockSpec((1, blk, cols), lambda c, h, i, s: (c, h * n + i, 0)),
        own[0].size, "widen", moved=12 * own[0].size,
    )


TILE = (128, 512)


def wide_kernel(count, adds, *refs):
    place, refs = refs[0], refs[1:]
    lhs, rhs = refs[:count], refs[count : 2 * count]
    total = refs[-1]
    a = 0.0
    for x, y in zip(lhs, rhs):
        a += dot(x[...], y[...].reshape(y.shape[-2:]), TN)
    total[...] = a.reshape(total.shape)
    add = refs[2 * count] if adds else None
    outs = refs[-5:-1] if adds else refs[-2:-1]
    x, y = place[1], place[2]
    for c in range(2):
        for a_rel in range(2):
            for b_rel in range(2):
                a_abs = a_rel ^ (x if c == 0 else y)
                b_abs = b_rel ^ (y if c == 0 else x)
                k = 4 * c + 2 * a_abs + b_abs
                for t in range(total.shape[2] // TILE[1]):
                    at = slice(TILE[1] * t, TILE[1] * (t + 1))
                    v = total[k, :, at]
                    if adds:
                        v = v + add[c, a_rel, b_rel, t].astype(F32)
                        outs[2 * c + a_rel][b_rel, t] = v.astype(BF)
                    else:
                        outs[0][c, a_rel, b_rel, t] = v.astype(BF)


def dense_kernel(count, adds, *refs):
    place, refs = refs[0], refs[1:]
    lhs, rhs = refs[:count], refs[count : 2 * count]
    total = refs[-1]
    a = 0.0
    for x, y in zip(lhs, rhs):
        a += dot(x[...], y[...], TN)
    for rb in range(2):
        for t in range(4):
            total[4 * rb + t] = a[128 * rb : 128 * (rb + 1), TILE[1] * t : TILE[1] * (t + 1)]
    add = refs[2 * count] if adds else None
    outs = refs[-5:-1] if adds else refs[-2:-1]
    x, y = place[1], place[2]
    for c in range(2):
        for a_rel in range(2):
            for b_rel in range(2):
                a_abs = a_rel ^ (x if c == 0 else y)
                b_abs = b_rel ^ (y if c == 0 else x)
                v = total[4 * c + 2 * a_abs + b_abs]
                if adds:
                    v = v + add[c, a_rel, b_rel, 0].astype(F32)
                    outs[2 * c + a_rel][b_rel, 0] = v.astype(BF)
                else:
                    outs[0][c, a_rel, b_rel, 0] = v.astype(BF)


def wide_part(kind, tiles, offset, place, lhs, rhs, add, base):
    rows, depth = lhs[0].shape
    if kind == "qkv":
        grid, step_tiles, cols = (3,), 1, 512
        rhs_spec = pl.BlockSpec((1, rows, cols), lambda n, h: (n, 0, 0))
    elif kind == "dense":
        grid, step_tiles, cols = (1,), 1, 2048
        rhs_spec = pl.BlockSpec((rows, cols), lambda n, h: (0, 0))
    else:
        step_tiles = 2 if offset % 2 == 0 else 1
        cols = 512 * step_tiles
        grid = (rhs[0].shape[1] // cols,)
        rhs_spec = pl.BlockSpec((rows, cols), lambda n, h: (0, n))
    lhs_spec = pl.BlockSpec((rows, depth // 2), lambda n, h: (0, h[0]))
    first = offset // step_tiles
    one = pl.BlockSpec((2, 2, 2, step_tiles) + TILE, lambda n, h: (0, 0, 0, first + n, 0, 0))
    four = pl.BlockSpec((2, step_tiles) + TILE, lambda n, h: (0, first + n, 0, 0))
    ins = [*lhs, *rhs]
    specs = [lhs_spec] * len(lhs) + [rhs_spec] * len(rhs)
    if add is None:
        outs, out_specs = [sds((2, 2, 2, tiles) + TILE, BF)], [one]
    else:
        ins.append(add)
        specs.append(one)
        outs, out_specs = [sds((2, tiles) + TILE, BF)] * 4, [four] * 4
    aliases = {}
    if base is not None:
        for i, b in enumerate(base):
            aliases[1 + len(ins)] = i
            ins.append(b)
            specs.append(pl.BlockSpec(memory_space=pl.ANY))
    kernel = dense_kernel if kind == "dense" else wide_kernel
    args = (len(lhs), add is not None)
    width = 512 if kind == "dense" else cols

    def body(*refs):
        if base is not None:
            cutoff = 1 + len(ins) - len(base)
            refs = refs[:cutoff] + refs[1 + len(ins) :]
        kernel(*args, *refs)

    planes = rhs[0].size // rows
    return pl.pallas_call(
        body,
        grid_spec=pltpu.PrefetchScalarGridSpec(
            num_scalar_prefetch=1, grid=grid, in_specs=specs, out_specs=out_specs,
            scratch_shapes=[pltpu.VMEM((8, 128, width), F32)],
        ),
        out_shape=outs,
        input_output_aliases=aliases,
        name="wide_" + kind,
        cost_estimate=pl.CostEstimate(
            flops=len(lhs) * rows * depth * planes,
            bytes_accessed=nbytes(*lhs) // 2 + nbytes(*rhs) + depth * planes * 2,
            transcendentals=0,
        ),
        compiler_params=pltpu.CompilerParams(vmem_limit_bytes=VMEM_LIMIT),
    )(place, *ins)


def group_half(parts, place, add=None):
    tiles = sum(p[1] for p in parts)
    base, offset = None, 0
    for kind, count, lhs, rhs in parts:
        base = wide_part(kind, tiles, offset, place, lhs, rhs, add, base)
        offset += count
    return base


def plus(*xs):
    return sum(x.astype(F32) for x in xs).astype(BF)


def hop(x, axis_bit):
    return lax.ppermute(x, "ctx", [(i, i ^ axis_bit) for i in range(4)])


def hop_in(x, axis_bit, layer):
    pairs = [(4 * layer + i, 4 * layer + (i ^ axis_bit)) for i in range(4)]
    return lax.ppermute(x, ("section", "ctx"), pairs)


def reduce_group(parts, layer, keep, send, order):
    base = group_half(order(parts), send)
    got = swap_sections(base[0])
    yield base[0]
    k0, s0, k1, s1 = group_half(order(parts), keep, got)
    r0, r1 = hop(s0, 1), hop(s1, 2)
    yield k0
    t0, t1 = plus(k0[1], r0[1]), plus(k1[1], r1[1])
    q0, q1 = hop(t0, 2), hop(t1, 1)
    yield t0
    f = jnp.stack([plus(k0[0], r0[0], q0), plus(k1[0], r1[0], q1)])
    other = lax.ppermute(f, "section", [(1 - layer, layer)])
    yield f
    full = jnp.stack([f, other] if layer == 0 else [other, f], axis=1)
    fx, fy = hop_in(full, 1, layer), hop_in(full, 2, layer)
    yield full
    d0, d1 = hop_in(fy[0], 1, layer), hop_in(fx[1], 2, layer)
    yield full, fx, fy, d0, d1


def widen_group_kernel(kinds, counts, *refs):
    sec = refs[0]
    step = pl.program_id(0)
    ins = refs[2:12]
    outs = refs[12:]
    starts = (0, 4, 8, 12, 14, 16)

    for layer in (0, 1):
        for k in range(5):
            src = ins[5 * layer + k]

            @pl.when((sec[0] == layer) & (step >= starts[k]) & (step < starts[k + 1]))
            def _(src=src):
                offset = 0
                for kind, count, out in zip(kinds, counts, outs):
                    for t in range(count):
                        tile = src[0, 0, offset + t].astype(F32)
                        if kind == "qkv":
                            out[t] = tile
                        elif kind == "dense":
                            out[...] = tile
                        else:
                            out[:, TILE[1] * t : TILE[1] * (t + 1)] = tile
                    offset += count


def widen_group(parts, sec, order, pieces):
    kinds = tuple(p[0] for p in parts)
    counts = tuple(p[1] for p in parts)
    tiles = sum(counts)
    specs, ins = [], []
    for layer in (0, 1):
        start = 0
        for piece in pieces[layer]:
            arr = piece.reshape((-1, 1, tiles) + TILE)
            n = arr.shape[0]

            def index_map(i, s, o, layer=layer, start=start, n=n):
                at = jnp.clip(i - start, 0, n - 1)
                return (jnp.where(s[0] == layer, at, 0), 0, 0, 0, 0)

            ins.append(arr)
            specs.append(pl.BlockSpec((1, 1, tiles) + TILE, index_map))
            start += n
    outs, out_specs = [], []
    for kind, count in zip(kinds, counts):
        if kind == "qkv":
            outs.append(sds((3, 2048, 512), F32))
            out_specs.append(pl.BlockSpec((3, 128, 512), lambda i, s, o: (0, o[i], 0)))
        elif kind == "dense":
            outs.append(sds((512, 2048), F32))
            out_specs.append(
                pl.BlockSpec((128, 512), lambda i, s, o: (o[i] // 4, o[i] % 4))
            )
        else:
            outs.append(sds((2048, 2048), F32))
            out_specs.append(pl.BlockSpec((128, 2048), lambda i, s, o: (o[i], 0)))
    return pl.pallas_call(
        functools.partial(widen_group_kernel, kinds, counts),
        grid_spec=pltpu.PrefetchScalarGridSpec(
            num_scalar_prefetch=2, grid=(16,), in_specs=specs, out_specs=out_specs
        ),
        out_shape=outs,
        name="widen_group",
        cost_estimate=pl.CostEstimate(
            flops=0, bytes_accessed=6 * 16 * tiles * 128 * 512, transcendentals=0
        ),
        compiler_params=pltpu.CompilerParams(vmem_limit_bytes=VMEM_LIMIT),
    )(sec, order, *ins)


def class_order(at_x, at_y):
    order = []
    for colours, dx, dy in (
        ((0, 1), 0, 0), ((0, 1), 1, 0), ((0, 1), 0, 1), ((0,), 1, 1), ((1,), 1, 1),
    ):
        for c in colours:
            for h in (0, 1):
                x, y = at_x ^ dx, at_y ^ dy
                a, b = (x, y) if c == 0 else (y, x)
                order.append(8 * h + 4 * c + 2 * a + b)
    return jnp.stack(order).astype(jnp.int32)


def swap_sections(x):
    return lax.ppermute(x, "section", [(0, 1), (1, 0)])


def butterfly(x, axis):
    length, bit = lax.axis_size(axis), 1
    while bit < length:
        x = x + lax.ppermute(x, axis, [(i, i ^ bit) for i in range(length)])
        bit *= 2
    return x


def shift_ctx(x, by):
    length = lax.axis_size("ctx")
    return lax.ppermute(
        x, "ctx", [(i, i + by) for i in range(length) if 0 <= i + by < length]
    )


def rope_tables(positions, width):
    half = ROT // 2
    frequency = 10000.0 ** (-(2.0 * jnp.arange(half, dtype=F32)) / ROT)
    angles = positions.astype(F32)[:, None] * frequency[None, :]
    c, s = jnp.cos(angles), jnp.sin(angles)
    zero = jnp.zeros_like(c)
    one = jnp.ones_like(c)

    def lay(*parts):
        head = jnp.concatenate(parts, axis=1)
        return jnp.tile(head, (1, width // HEAD))

    return lay(c, c, one, one), lay(s, zero, zero, zero), lay(zero, s, zero, zero)


def on_device(
    inputs,
    segments,
    cotangent,
    ln_gain,
    ln_bias,
    qkv_weight,
    qkv_bias,
    dense_weight,
    fc1_weight,
    fc1_bias,
    fc2_weight,
    out_bias,
):
    sections = lax.axis_size("section")
    section = lax.axis_index("section")
    ctx_id = lax.axis_index("ctx")
    ctx = lax.axis_size("ctx")
    batches, r, width = inputs.shape
    rows = r * lax.axis_size("tp")
    total_rows = rows * ctx
    local = qkv_weight.shape[3]
    hidden = fc1_weight.shape[2]
    mine = batches // sections
    back = (total_rows // 2) // rows
    blocks = min(back, ctx - 1) + 1
    first_mb = section * mine
    layers = (0, 1)
    square = (ctx, local, hidden, width) == (4, 512, 2048, 2048)
    at_x, at_y = ctx_id % 2, ctx_id // 2

    small = jnp.concatenate(
        [ln_gain[0], ln_bias[0], out_bias[0], qkv_bias[0].reshape(-1), fc1_bias[0]]
    )
    small_other = swap_sections(small)
    w_own = (qkv_weight[0], fc1_weight[0], dense_weight[0], fc2_weight[0])
    ready, _ = lax.optimization_barrier((w_own, small_other))
    w_other = tuple(swap_sections(w) for w in ready)
    sel, gain, shift, obias, qkv_b, fc1_b = [], [], [], [], [], []
    for layer in layers:
        sel.append((section != layer).astype(jnp.int32).reshape(1))
        v = jnp.where(section == layer, small, small_other).astype(F32)
        gain.append(v[:width].reshape(1, width))
        shift.append(v[width : 2 * width].reshape(1, width))
        obias.append(v[2 * width : 3 * width].reshape(1, width))
        qkv_b.append(v[3 * width : 3 * width + 3 * local].reshape(3, 1, local))
        fc1_b.append(v[3 * width + 3 * local :].reshape(1, hidden))

    positions = ctx_id * rows + jnp.arange(rows, dtype=jnp.int32)
    tables = rope_tables(positions, PAIR)

    docs = lax.dynamic_slice_in_dim(segments, first_mb, mine, 0)
    padded = jnp.pad(docs, ((0, 0), ((blocks - 1) * rows, 0)), constant_values=-1)
    window = lax.dynamic_slice_in_dim(padded, ctx_id * rows, blocks * rows, 1)
    window = window.reshape(mine, blocks, rows)[:, ::-1]
    drow = [window[m, 0].reshape(1, rows) for m in range(mine)]
    dcol = [window[m].reshape(blocks * rows, 1) for m in range(mine)]

    x_in = lax.dynamic_slice_in_dim(inputs, first_mb, mine, 0)
    g_in = lax.dynamic_slice_in_dim(cotangent, first_mb, mine, 0)

    def gather(v):
        return lax.all_gather(v, "tp", axis=0, tiled=True)

    def scatter(v):
        return lax.psum_scatter(v, "tp", scatter_dimension=0, tiled=True)

    qw, fw, dw, ow = zip(w_own, w_other)
    last = [None]

    def after(v):
        if last[0] is None:
            return v
        return lax.optimization_barrier((v, last[0]))[0]

    def mark(out):
        last[0] = jax.tree.leaves(out)[0]
        return out

    S = {}

    def project_step(l, m):
        q, kv = mark(project(sel[l], after(S["full", l, m]), *qw, qkv_b[l], tables))
        S["q", l, m] = q
        S["kvs", l, m] = [kv] + [shift_ctx(kv, j) for j in range(1, blocks)]

    def expand_step(l, m):
        S["gelu", l, m], S["slope", l, m] = mark(
            expand(sel[l], after(S["full", l, m]), *fw, fc1_b[l])
        )

    def attend_step(l, m):
        S["att", l, m], S["lse", l, m] = mark(
            attend(after(S["q", l, m]), S["kvs", l, m], drow[m], dcol[m])
        )

    def contract_step(l, m):
        part = mark(
            contract(sel[l], after(S["att", l, m]), S["gelu", l, m], dw[0], ow[0], dw[1], ow[1])
        )
        S["branch", l, m] = scatter(part)

    def next_step(l, m):
        S["x", l + 1, m], normed = mark(
            norm_next(after(S["x", l, m]), S["branch", l, m], obias[l], gain[l + 1], shift[l + 1])
        )
        S["full", l + 1, m] = gather(normed)

    def attn_grad_step(l, m):
        ga = mark(spread_attn(sel[l], after(S["gfull", l, m]), *dw))
        out = mark(
            attend_back(
                after(S["q", l, m]), S["kvs", l, m], ga, S["lse", l, m], drow[m], dcol[m], tables
            )
        )
        S["gq", l, m] = out[:2]
        S["got", l, m] = [shift_ctx(out[1 + j], -j) for j in range(1, blocks)]

    def up_grad_step(l, m):
        S["up", l, m], S["bu", l, m] = mark(
            spread_up(sel[l], after(S["gfull", l, m]), *ow, S["slope", l, m])
        )

    def join_step(l, m):
        gq, own = S["gq", l, m]
        S["qkv", l, m] = mark(join(after(gq), own, S["got", l, m], tables))

    def gather_step(l, m):
        part, S["bq", l, m] = mark(
            gather_grad(
                sel[l], after(S["qkv", l, m]), S["up", l, m], qw[0], fw[0], qw[1], fw[1]
            )
        )
        S["gn", l, m] = scatter(part)

    def back_step(l, m):
        S["gx", l, m], S["sums", l, m] = mark(
            norm_back(after(S["x", l, m]), S["gn", l, m], S["g", l, m], gain[l])
        )
        if l > 0:
            S["g", l - 1, m] = S["gx", l, m]
            S["gfull", l - 1, m] = gather(S["gx", l, m])

    def each(name, l):
        return [S[name, l, m] for m in range(mine)]

    keep_half = section.astype(jnp.int32)
    place_keep = jnp.stack([keep_half, at_x, at_y]).astype(jnp.int32)
    place_send = jnp.stack([1 - keep_half, at_x, at_y]).astype(jnp.int32)

    def ordered(parts):
        (kind, count, lhs, rhs), *rest = parts
        return [(kind, count, [after(lhs[0]), *lhs[1:]], rhs), *rest]

    def out_parts(l):
        g = each("gfull", l)
        return (("fc2", 4, each("gelu", l), g), ("dense", 1, each("att", l), g))

    def in_parts(l):
        full = each("full", l)
        return (("fc1", 4, full, each("up", l)), ("qkv", 3, full, each("qkv", l)))

    groups = {}

    def group_step(l, k):
        if not square:
            return
        if (l, k) not in groups:
            parts = (out_parts, in_parts)[k](l)
            groups[l, k] = reduce_group(parts, l, place_keep, place_send, ordered)
        S["group", l, k] = next(groups[l, k])
        mark(S["group", l, k])

    for m in range(mine):
        S["x", 0, m] = x_in[m]
        S["full", 0, m] = gather(mark(norm_first(after(x_in[m]), gain[0], shift[0])))
    for m in range(mine):
        project_step(0, m)
        if m == 0:
            expand_step(0, 0)
    for m in range(mine):
        if m > 0:
            expand_step(0, m)
        attend_step(0, m)
        contract_step(0, m)
    for m in range(mine):
        next_step(0, m)
    held = lax.optimization_barrier((g_in, S["full", 1, mine - 1]))[0]
    for m in range(mine):
        S["g", 1, m] = g_in[m]
        S["gfull", 1, m] = gather(held[m])
    for m in range(mine):
        project_step(1, m)
        if m == 0:
            expand_step(1, 0)
    for m in range(mine):
        if m > 0:
            expand_step(1, m)
        attend_step(1, m)

    group_step(1, 0)
    attn_grad_step(1, 0)
    group_step(1, 0)
    for m in range(1, mine):
        attn_grad_step(1, m)
    for m in range(mine):
        up_grad_step(1, m)
        join_step(1, m)
        gather_step(1, m)
        group_step(1, 0) if m < 2 else None
    group_step(1, 1)
    group_step(1, 0)
    group_step(1, 1)
    for m in range(mine):
        back_step(1, m)
    for m in range(mine):
        contract_step(1, m)
    group_step(1, 0)
    attn_grad_step(0, 0)
    up_grad_step(0, 0)
    group_step(1, 1)
    for m in range(1, mine):
        attn_grad_step(0, m)
    group_step(0, 0)
    join_step(0, 0)
    gather_step(0, 0)
    group_step(0, 0)
    for m in range(1, mine):
        up_grad_step(0, m)
        join_step(0, m)
        gather_step(0, m)
    group_step(1, 1)
    group_step(0, 1)
    group_step(1, 1)
    group_step(0, 1)
    for m in range(mine):
        back_step(0, m)
    group_step(0, 0)
    group_step(0, 0)
    group_step(0, 1)
    group_step(1, 1)
    group_step(0, 0)
    group_step(0, 1)
    group_step(0, 0)
    group_step(0, 1)
    group_step(0, 1)

    outs = [jnp.stack(each("x", 1)), None]
    outs[1] = jnp.stack(
        [
            (x.astype(F32) + b.astype(F32) + obias[1]).astype(BF)
            for x, b in zip(each("x", 1), each("branch", 1))
        ]
    )
    gin = [jnp.stack(each("gx", l)) for l in layers]
    sums = [sum(each("sums", l)) for l in layers]
    biases = [
        jnp.concatenate([sum(each("bq", l)).reshape(-1), sum(each("bu", l)).reshape(-1)])
        for l in layers
    ]
    halves = {}
    for l in layers:
        if square:
            halves[l] = [S["group", l, k] for k in range(2)]
        else:
            halves[l] = []
            for _, _, lhs, rhs in out_parts(l) + in_parts(l):
                rhs = [v.reshape((-1,) + v.shape[-2:]) for v in rhs]
                got = swap_sections(weight_half(place_send[:1], lhs, rhs))
                halves[l].append(
                    lax.psum(weight_half(place_keep[:1], lhs, rhs, got), "ctx")
                )

    def to_owner(pair_of):
        moved = swap_sections(jnp.where(section == 0, pair_of[1], pair_of[0]))
        own = jnp.where(section == 0, pair_of[0], pair_of[1])
        return jnp.where(
            section == 0,
            jnp.concatenate([own, moved], axis=0),
            jnp.concatenate([moved, own], axis=0),
        )

    layer_out = to_owner(outs)
    grad_in = to_owner([gin[0], gin[1]])

    final = []
    if square:
        order = class_order(at_x, at_y)
        for k, parts in enumerate((out_parts(0), in_parts(0))):
            final += widen_group(
                parts, place_keep[:1], order, [halves[layer][k] for layer in layers]
            )
    else:
        for k in range(4):
            own = [halves[layer][k] for layer in layers]
            got = [
                lax.ppermute(own[layer], "section", [(1 - layer, layer)])
                for layer in layers
            ]
            final.append(widen(place_keep[:1], own, got))
    fc2_g, dense_g, fc1_g, qkv_gr = final
    dense_g = dense_g.reshape(1, local, width)
    fc2_g = fc2_g.reshape(1, hidden, width)
    fc1_g = fc1_g.reshape(1, width, hidden)

    flat = [jnp.concatenate([sums[l].reshape(-1), biases[l]]) for l in layers]
    total = jnp.where(section == 0, flat[0], flat[1]) + swap_sections(
        jnp.where(section == 0, flat[1], flat[0])
    )
    total = butterfly(total, "ctx")
    rowsum = butterfly(total[: 3 * width], "tp").reshape(3, width)
    bias_sum = total[3 * width :]

    return (
        layer_out[None],
        grad_in[None],
        rowsum[0][None],
        rowsum[1][None],
        qkv_gr[None],
        bias_sum[: 3 * local].reshape(3, local)[None],
        dense_g,
        fc1_g,
        bias_sum[3 * local :][None],
        fc2_g,
        rowsum[2][None],
    )


def solution(mesh):
    return jax.shard_map(
        on_device,
        mesh=mesh,
        in_specs=(
            P(None, ("ctx", "tp"), None),
            P(),
            P(None, ("ctx", "tp"), None),
            P("section", None),
            P("section", None),
            P("section", None, None, "tp"),
            P("section", None, "tp"),
            P("section", "tp", None),
            P("section", None, "tp"),
            P("section", "tp"),
            P("section", "tp", None),
            P("section", None),
        ),
        out_specs=(
            P("section", None, ("ctx", "tp"), None),
            P("section", None, ("ctx", "tp"), None),
            P("section", None),
            P("section", None),
            P("section", None, None, "tp"),
            P("section", None, "tp"),
            P("section", "tp", None),
            P("section", None, "tp"),
            P("section", "tp"),
            P("section", "tp", None),
            P("section", None),
        ),
        check_vma=False,
    )
```
